256 devices in a mesh: cfg: 2 (over core), tok: 128 (over y, z, x).
Axes of the slice: x: 4, y: 4, z: 8, core: 2. Of those that a mesh axis runs over, the one named last changes fastest.
Arguments:
- hidden_in: bfloat16 [24576, 1152], P('tok'), may hold values from -6 to 6
- noisy_latent: float32 [24576, 16], P('tok'), may hold values from -6 to 6
- piece_rows: int32 [16, 8], replicated, may hold values from 1 to 192, 1024 in all within a row
- modulation: float32 [2, 16, 8, 1152], P('cfg'), may hold values from -3 to 3
- qkv_weight: bfloat16 [128, 1152, 432], P('tok'), may hold values from -1 to 1, as said below
- proj_weight: bfloat16 [128, 1152, 144], P('tok'), may hold values from -1 to 1, as said below
- up_weight: bfloat16 [128, 1152, 576], P('tok'), may hold values from -1 to 1, as said below
- down_weight: bfloat16 [128, 1152, 576], P('tok'), may hold values from -1 to 1, as said below
- final_weight: bfloat16 [1152, 16], replicated, may hold values from -0.1875 to 0.1875
- guidance: float32 [16], replicated, may hold values from 1.5 to 4.5
- solver_coef: float32 [16, 2], replicated, may hold values from 0.3 to 1.2
Outputs:
- next_latent: float32 [24576, 16], P('tok')
- block_out: bfloat16 [2, 24576, 1152], P('cfg', 'tok')
The draws below stay inside these ranges and needn't reach their ends.
Inputs may be any that keep to these rules, and one draw needn't show every extreme that they name: Row l of piece_rows sums to 1024; in every row the largest entry is 192. `qkv_weight`: copy i equals copy i % 8. `proj_weight`: copy i equals copy i % 8. `up_weight`: copy i equals copy i % 8. `down_weight`: copy i equals copy i % 8.
All inputs are finite; a program needn't handle non-finite values.
Results may differ from the reference program's by a relative error of at most 0.008.
Values may be sent and summed in bfloat16 or wider, within the bound.
A program may use at most 64 MiB of HBM per device.

```python
import math
import jax
import jax.numpy as jnp
import numpy as np
from jax import lax

D = 1152
HEADS = 16
HEAD_DIM = 72
FF = 4608
OUTC = 16
GROUP = 8
LEN = 1024
CAP = 192
LATENTS = 16
SLOTS = 24576


def copy_blocks(full_cols, block_width):
    row_count = full_cols.shape[0]
    blocks = full_cols.reshape(row_count, GROUP, block_width).transpose(1, 0, 2)
    return jnp.tile(blocks, (LATENTS, 1, 1))


def drawn_matrix(key, rows, cols, fan_in):
    return jnp.clip(jnp.clip(jax.random.normal(key, (rows, cols), jnp.float32), -6.0, 6.0) * fan_in ** (-0.5), -1.0, 1.0)


def draw_qkv_weight(key, part):
    key_base = jax.random.fold_in(key, 11)
    base_cols = jnp.clip(jax.random.normal(key_base, (D, 3 * D), jnp.float32), -6.0, 6.0) * D ** (-0.5)
    full_cols = jnp.clip(base_cols, -1.0, 1.0)
    head_width = D // GROUP
    blocks = full_cols.reshape(D, 3, GROUP, head_width).transpose(2, 0, 1, 3).reshape(GROUP, D, 3 * head_width)
    return jnp.tile(blocks, (LATENTS, 1, 1)).astype(jnp.bfloat16)


def draw_proj_weight(key, part):
    return copy_blocks(drawn_matrix(jax.random.fold_in(key, 21), D, D, D), D // GROUP).astype(jnp.bfloat16)


def draw_up_weight(key, part):
    return copy_blocks(drawn_matrix(jax.random.fold_in(key, 31), D, FF, D), FF // GROUP).astype(jnp.bfloat16)


def draw_down_weight(key, part):
    return copy_blocks(drawn_matrix(jax.random.fold_in(key, 41), D, FF, FF), FF // GROUP).astype(jnp.bfloat16)


def block_scale(rng, extent, cuts, low, largest):
    factor_of = 1.0
    for dim, blocks in cuts:
        draws = jax.random.uniform(jax.random.fold_in(jax.random.fold_in(rng, 6), dim), (blocks,), jnp.float32, low / len(cuts), largest / len(cuts))
        factor_of = factor_of * jnp.repeat(jnp.exp(draws), extent[dim] // blocks).reshape((-1,) + (1,) * (len(extent) - 1 - dim))
    return factor_of


def split_up(count, total, bound, lean):
    portions = [(1 << 20) // math.isqrt(standing ** lean) + 1 for standing in range(2, count + 1)]
    rest, given = total - bound - (count - 1), [1] * (count - 1)
    while rest > 0:
        candidates = [i for i in range(count - 1) if given[i] < bound]
        pool, remaining = sum([portions[i] for i in candidates]), rest
        for i in candidates:
            extra = min(bound - given[i], max(1, remaining * portions[i] // pool), rest)
            given[i] = given[i] + extra
            rest = rest - extra
    return np.array([bound] + given)


def ragged(key, number_of, total, most, lean):
    if number_of == 2:
        one = jax.random.randint(key, (), max(1, total - most), min(most, total - 1) + 1)
        return jnp.stack([one, total - one])
    tallies = jnp.asarray(split_up(number_of, total, most, lean), jnp.int32)
    pairs = (number_of - 1) // 2
    donor, receiver = tallies[1:1 + 2 * pairs:2], tallies[2:2 + 2 * pairs:2]
    margin = jnp.minimum(donor - 1, most - receiver)
    moved = jax.random.randint(jax.random.fold_in(key, 1), (pairs,), 0, 1 << 20) % (margin + 1)
    tallies = tallies.at[1:1 + 2 * pairs:2].set(donor - moved).at[2:2 + 2 * pairs:2].set(receiver + moved)
    return tallies[jax.random.permutation(jax.random.fold_in(key, 2), number_of)]


def bell_draw(own_key, dims, scale, most, split=(), kind=jnp.bfloat16):
    values = scale * jax.random.normal(own_key, dims, jnp.float32)
    if split:
        values = values * block_scale(own_key, dims, split, -0.22, 0.18)
    return jnp.clip(values, -most, most).astype(kind)


def setup_inputs(seed: int = 0) -> dict:
    streams_of = jax.random.split(jax.random.key(seed), 12)
    hidden_in = bell_draw(streams_of[0], (SLOTS, D), 1.0, 6.0, ((0, 128),))
    noisy_latent = bell_draw(streams_of[1], (SLOTS, OUTC), 1.0, 6.0, ((0, 128),), jnp.float32)
    piece_rows = jax.vmap(lambda own: ragged(own, GROUP, LEN, CAP, 2))(jax.random.split(streams_of[2], LATENTS)).reshape((LATENTS, GROUP)).astype(jnp.int32)
    modulation = bell_draw(streams_of[3], (2, LATENTS, 8, D), 0.6, 3.0, ((0, 2),), jnp.float32)
    qkv_weight = draw_qkv_weight(jax.random.fold_in(streams_of[11], 71), 0)
    proj_weight = draw_proj_weight(jax.random.fold_in(streams_of[11], 71), 0)
    up_weight = draw_up_weight(jax.random.fold_in(streams_of[11], 71), 0)
    down_weight = draw_down_weight(jax.random.fold_in(streams_of[11], 71), 0)
    final_weight = bell_draw(streams_of[8], (D, OUTC), D ** -0.5, 0.1875)
    guidance = jnp.clip(jax.random.uniform(streams_of[9], (LATENTS,), jnp.float32, 1.5, 4.5), 1.5, 4.5)
    solver_coef = jnp.clip(jax.random.uniform(streams_of[10], (LATENTS, 2), jnp.float32, 0.3, 1.2), 0.3, 1.2)
    return {"hidden_in": hidden_in, "noisy_latent": noisy_latent, "piece_rows": piece_rows, "modulation": modulation, "qkv_weight": qkv_weight, "proj_weight": proj_weight, "up_weight": up_weight, "down_weight": down_weight, "final_weight": final_weight, "guidance": guidance, "solver_coef": solver_coef}


def layer_norm(values):
    center = values - lax.optimization_barrier(jnp.mean(values, axis=-1, keepdims=True))
    spread = lax.optimization_barrier(jnp.mean(center * center, axis=-1, keepdims=True))
    return center / jnp.sqrt(spread + 1e-06)

def modulate(values, shift_vec, scale_vec):
    return layer_norm(values) * (1.0 + scale_vec) + shift_vec

def latent_block(rows_now, valid_now, factors, qkv_weight, proj_weight, up_weight, down_weight, final_weight):
    row_count = rows_now.shape[0]
    inv_root = HEAD_DIM ** (-0.5)
    inputs = rows_now.astype(jnp.float32)
    attn_in = modulate(inputs, factors[0], factors[1]).astype(jnp.bfloat16)
    projected = jnp.dot(attn_in, qkv_weight, preferred_element_type=jnp.float32).astype(jnp.bfloat16)
    split_heads = projected.reshape(row_count, 3, HEADS, HEAD_DIM).transpose(1, 2, 0, 3)

    def one_head(operands):
        query_head, key_head, value_head = operands
        scores = jnp.dot(query_head, key_head.T, preferred_element_type=jnp.float32) * inv_root
        scores = jnp.where(valid_now[None, :], scores, -1e+30)
        row_peak = lax.optimization_barrier(jnp.max(scores, axis=-1, keepdims=True))
        exp_scores = jnp.exp(scores - row_peak)
        attn_probs = (exp_scores / lax.optimization_barrier(jnp.sum(exp_scores, axis=-1, keepdims=True))).astype(jnp.bfloat16)
        return jnp.dot(attn_probs, value_head, preferred_element_type=jnp.float32).astype(jnp.bfloat16)
    heads_out = lax.map(one_head, (split_heads[0], split_heads[1], split_heads[2]))
    heads_flat = heads_out.transpose(1, 0, 2).reshape(row_count, HEADS * HEAD_DIM)
    attn_out = jnp.dot(heads_flat, proj_weight.T, preferred_element_type=jnp.float32)
    residual_mid = inputs + factors[2] * attn_out
    mlp_input = modulate(residual_mid, factors[3], factors[4]).astype(jnp.bfloat16)
    hidden_units = jax.nn.gelu(jnp.dot(mlp_input, up_weight, preferred_element_type=jnp.float32), approximate=True).astype(jnp.bfloat16)
    mlp_out = jnp.dot(hidden_units, down_weight.T, preferred_element_type=jnp.float32)
    block_rows = (residual_mid + factors[5] * mlp_out).astype(jnp.bfloat16)
    block_rows = jnp.where(valid_now[:, None], block_rows, jnp.zeros_like(block_rows))
    final_in = modulate(block_rows.astype(jnp.float32), factors[6], factors[7]).astype(jnp.bfloat16)
    noise_pred = jnp.dot(final_in, final_weight, preferred_element_type=jnp.float32)
    return (block_rows, noise_pred)

def reference(hidden_in, noisy_latent, piece_rows, modulation, qkv_weight, proj_weight, up_weight, down_weight, final_weight, guidance, solver_coef):
    head_width = D // GROUP
    full_qkv = qkv_weight[:GROUP].reshape(GROUP, D, 3, head_width).transpose(1, 2, 0, 3).reshape(D, 3 * D)
    full_proj = proj_weight[:GROUP].transpose(1, 0, 2).reshape(D, D)
    full_up = up_weight[:GROUP].transpose(1, 0, 2).reshape(D, FF)
    full_down = down_weight[:GROUP].transpose(1, 0, 2).reshape(D, FF)
    latent_rows = hidden_in.reshape(LATENTS, GROUP * CAP, D)
    slot_pos = jnp.arange(CAP, dtype=jnp.int32)
    valid_rows = (slot_pos[None, None, :] < piece_rows[:, :, None]).reshape(LATENTS, GROUP * CAP)

    def per_latent(operands):
        rows_now, valid_now, cond_factors, uncond_factors = operands
        cond_block, cond_pred = latent_block(rows_now, valid_now, cond_factors, full_qkv, full_proj, full_up, full_down, final_weight)
        uncond_block, uncond_pred = latent_block(rows_now, valid_now, uncond_factors, full_qkv, full_proj, full_up, full_down, final_weight)
        return (cond_block, uncond_block, cond_pred, uncond_pred)
    cond_block, uncond_block, cond_pred, uncond_pred = lax.map(per_latent, (latent_rows, valid_rows, modulation[0], modulation[1]))
    scale_now = guidance[:, None, None]
    guided = scale_now * cond_pred + (1.0 - scale_now) * uncond_pred
    coef_keep = solver_coef[:, 0][:, None, None]
    coef_noise = solver_coef[:, 1][:, None, None]
    stepped = coef_keep * noisy_latent.reshape(LATENTS, GROUP * CAP, OUTC) - coef_noise * guided
    next_latent = jnp.where(valid_rows[:, :, None], stepped, jnp.zeros_like(stepped)).reshape(SLOTS, OUTC)
    block_out = jnp.stack([cond_block, uncond_block]).reshape(2, SLOTS, D)
    return (next_latent, block_out)
```

```python
import jax
import jax.numpy as jnp
from jax import lax
from jax.experimental import pallas as pl
from jax.experimental.pallas import tpu as pltpu
from jax.sharding import PartitionSpec as P

MESH = pl.DeviceIdType.MESH
F32 = jnp.float32
BF16 = jnp.bfloat16
HD = 72
GROUP = 8
LANE = 128
ROWS = 192
D = 1152
UNITS = 576
CHUNK = 256
RCH = 2
EXP_SCALE = HD**-0.5 * 1.4426950408889634

INNER, OUTER, ZED = 1, 3, 4
WSLOT = {0: 0, 4: 1, 3: 2, 7: 3}


def nt(a, b):
    return lax.dot_general(a, b, (((1,), (1,)), ((), ())), preferred_element_type=F32)


def nn(a, b):
    return jnp.dot(a, b, preferred_element_type=F32)


def norm(v):
    center = v - jnp.mean(v, axis=-1, keepdims=True)
    spread = jnp.mean(center * center, axis=-1, keepdims=True)
    return center * lax.rsqrt(spread + 1e-06)


def kernel(
    hid_hbm, lat_ref, counts_ref, mod_hbm, wq_hbm, wp_hbm, wu_hbm, wd_hbm, fw_ref, gd_ref, sc_ref,
    out_lat, out_blk,
    hd, mod, wq_raw, wp_raw, wu_raw, wd_raw, wq, wp, wu, wd,
    qb, kb, vb, hs, hb, xb, acc, res, rs, rr, ps, pr,
    lsem, ssem, rsem,
):
    tok = lax.axis_index("tok")
    half = lax.axis_index("cfg")
    latent = tok // GROUP
    member = tok % GROUP
    z = (tok // 4) % 8
    zo = jnp.where(z % 2 == 1, (z + 1) % 8, (z + 7) % 8)
    zed_out = tok + (zo - z) * 4

    def flip(slot):
        bit0 = tok % 2
        bit1 = (tok // 2) % 2
        bit2 = (tok // 4) % 2
        s0, s1, s2 = slot % 2, (slot // 2) % 2, (slot // 4) % 2
        return tok + s0 * (1 - 2 * bit0) + 2 * s1 * (1 - 2 * bit1) + 4 * s2 * (1 - 2 * bit2)

    inner = {"cfg": half, "tok": flip(INNER)}
    outer = {"cfg": half, "tok": flip(OUTER)}
    zin = {"cfg": half, "tok": flip(ZED)}
    zout = {"cfg": half, "tok": zed_out}
    sib = {"cfg": 1 - half, "tok": tok}

    loads = [
        pltpu.make_async_copy(hid_hbm, hd.at[0], lsem.at[0]),
        pltpu.make_async_copy(wp_hbm.at[0], wp_raw, lsem.at[1]),
        pltpu.make_async_copy(wu_hbm.at[0], wu_raw, lsem.at[2]),
        pltpu.make_async_copy(wd_hbm.at[0], wd_raw, lsem.at[3]),
        pltpu.make_async_copy(wq_hbm.at[0], wq_raw, lsem.at[4]),
        pltpu.make_async_copy(mod_hbm.at[0, latent], mod, lsem.at[5]),
    ]
    for load in loads:
        load.start()

    barrier = pltpu.get_barrier_semaphore()
    peers = [{"cfg": half, "tok": flip(s)} for s in range(1, GROUP)] + [zout, sib]
    for peer in peers:
        pl.semaphore_signal(barrier, inc=1, device_id=peer, device_id_type=MESH)
    pl.semaphore_wait(barrier, len(peers))

    sent = []
    number = [0]

    def plan(src, dst, device):
        index = number[0]
        number[0] += 1
        return pltpu.make_async_remote_copy(
            src_ref=src, dst_ref=dst, send_sem=ssem.at[index], recv_sem=rsem.at[index],
            device_id=device, device_id_type=MESH,
        )

    def send(src, dst, device):
        copy = plan(src, dst, device)
        copy.start()
        sent.append(copy)
        return copy

    def rows_of(slot, part=None):
        if part is None:
            return hd.at[slot, pl.ds(pl.multiple_of(half * 96, 16), 96)]
        return hd.at[slot, pl.ds(pl.multiple_of(half * 96 + part * 48, 16), 48)]

    def proj_of(slot):
        return wp.at[2 * slot + half, pl.ds(0, 80)]

    def mlp_of(ref, slot):
        return ref.at[pl.ds(pl.multiple_of(WSLOT[slot] * UNITS + half * 288, 16), 288)]

    def to_sib(ref):
        return send(ref, ref, sib)

    loads[0].wait()
    h_outer = send(rows_of(0), rows_of(OUTER), outer)
    h_inner = send(rows_of(0), rows_of(INNER), inner)
    h_zed = send(rows_of(0), rows_of(ZED), zin)

    wp[:, 80:LANE] = jnp.zeros((2 * GROUP, LANE - 80, D), BF16)
    loads[1].wait()
    row = lax.broadcasted_iota(jnp.int32, (160, 2 * HD), 0)
    col = lax.broadcasted_iota(jnp.int32, (160, 2 * HD), 1)
    pick = ((row < HD) & (col == row)) | ((row >= 80) & (row < 80 + HD) & (col == row - 8))
    own_proj = nt(jnp.where(pick, 1.0, 0.0).astype(BF16), wp_raw[...]).astype(BF16)
    wp[0, 0:80] = own_proj[0:80]
    wp[1, 0:80] = own_proj[80:160]

    loads[2].wait()
    loads[3].wait()

    @pl.loop(0, 2)
    def _(step):
        row = lax.broadcasted_iota(jnp.int32, (288, UNITS), 0) + step * 288
        col = lax.broadcasted_iota(jnp.int32, (288, UNITS), 1)
        pick = jnp.where(row == col, 1.0, 0.0).astype(BF16)
        at = pl.ds(pl.multiple_of(step * 288, 16), 288)
        wu[at] = nt(pick, wu_raw[...]).astype(BF16)
        wd[at] = nt(pick, wd_raw[...]).astype(BF16)

    p_outer = send(proj_of(0), proj_of(OUTER), outer)
    u_outer = send(mlp_of(wu, 0), mlp_of(wu, OUTER), outer)
    d_outer = send(mlp_of(wd, 0), mlp_of(wd, OUTER), outer)
    p_zed = send(proj_of(0), proj_of(ZED), zout)
    d_zed = send(mlp_of(wd, 0), mlp_of(wd, ZED), zout)

    loads[4].wait()
    loads[5].wait()
    row = lax.broadcasted_iota(jnp.int32, (6 * HD, 6 * LANE), 0)
    col = lax.broadcasted_iota(jnp.int32, (6 * HD, 6 * LANE), 1)
    pick = (row == (col // LANE) * HD + col % LANE) & (col % LANE < HD)
    wq[...] = nn(wq_raw[...], jnp.where(pick, 1.0, 0.0).astype(BF16)).astype(BF16)

    lane = lax.broadcasted_iota(jnp.int32, (1, 2 * LANE), 1) % LANE
    one_lane = jnp.where(lane == HD, 1.0, 0.0)
    slot_row = lax.broadcasted_iota(jnp.int32, (ROWS, 1), 0)

    def project(slot):
        x = hd[slot].astype(F32)
        a = (norm(x) * (1.0 + mod[1:2]) + mod[0:1]).astype(BF16)
        y = nn(a, wq[...])
        count = counts_ref[latent, flip(slot) % GROUP]
        bias = jnp.where(slot_row < count, 0.0, -1e30)
        at = pl.ds(pl.multiple_of(slot * ROWS, 16), ROWS)
        qb[at] = (y[:, 0:256] + one_lane).astype(BF16)
        kb[at] = (y[:, 256:512] + one_lane * bias).astype(BF16)
        vb[at] = (y[:, 512:768] + one_lane).astype(BF16)

    def project_all(slots):
        first, stride, count = slots

        @pl.loop(0, count)
        def _(i):
            project(first + i * stride)

    h_outer.wait_recv()
    h_i2 = send(rows_of(OUTER), rows_of(2), inner)
    h_z7 = send(rows_of(OUTER), rows_of(7), zin)
    s3 = to_sib(rows_of(OUTER))
    h_zed.wait_recv()
    h_i5 = send(rows_of(ZED, 0), rows_of(5, 0), inner)
    s4 = to_sib(rows_of(ZED))
    h_inner.wait_recv()
    h_z5 = send(rows_of(INNER, 1), rows_of(5, 1), zin)
    s1 = to_sib(rows_of(INNER))

    project_all((0, 1, 1))
    s3.wait_recv()
    s4.wait_recv()
    project_all((3, 1, 2))

    h_z7.wait_recv()
    h_i6 = send(rows_of(7, 0), rows_of(6, 0), inner)
    s7 = to_sib(rows_of(7))
    h_i2.wait_recv()
    h_z6 = send(rows_of(2, 1), rows_of(6, 1), zin)
    s2 = to_sib(rows_of(2))
    p_inner = send(proj_of(0), proj_of(INNER), inner)
    u_zed = send(mlp_of(wu, 0), mlp_of(wu, ZED), zin)

    s1.wait_recv()
    s2.wait_recv()
    project_all((1, 1, 2))
    h_i5.wait_recv()
    h_z5.wait_recv()
    s5 = to_sib(rows_of(5))

    p_outer.wait_recv()
    p_i2 = send(proj_of(OUTER), proj_of(2), inner)
    p_z7 = send(proj_of(OUTER), proj_of(7), zout)
    q3 = to_sib(proj_of(OUTER))
    p_zed.wait_recv()
    q4 = to_sib(proj_of(ZED))

    s7.wait_recv()
    s5.wait_recv()
    project_all((5, 2, 2))
    h_i6.wait_recv()
    h_z6.wait_recv()
    s6 = to_sib(rows_of(6))
    p_inner.wait_recv()
    p_z5 = send(proj_of(INNER), proj_of(5), zout)
    q1 = to_sib(proj_of(INNER))
    s6.wait_recv()
    project_all((6, 1, 1))

    def attend(slot, out):
        at = pl.ds(pl.multiple_of(slot * ROWS, 16), ROWS)
        for head in range(2):
            lanes = pl.ds(head * LANE, LANE)
            scores = nt(qb[at, lanes], kb[:, lanes])
            peak = jnp.max(scores, axis=-1, keepdims=True)
            probs = jnp.exp2((scores - peak) * EXP_SCALE).astype(BF16)
            o = nn(probs, vb[:, lanes])
            out[slot, :, lanes] = (o / o[:, HD : HD + 1]).astype(BF16)

    base = number[0]
    number[0] += GROUP

    def head_copy(slot):
        return pltpu.make_async_remote_copy(
            src_ref=hs.at[slot], dst_ref=hb.at[slot], send_sem=ssem.at[base + slot], recv_sem=rsem.at[base + slot],
            device_id={"cfg": half, "tok": flip(slot)}, device_id_type=MESH,
        )

    def attend_all(low, high):
        @pl.loop(low, high)
        def _(i):
            slot = GROUP - i
            attend(slot, hs)
            head_copy(slot).start()

    attend_all(1, 5)
    p_i2.wait_recv()
    p_z6 = send(proj_of(2), proj_of(6), zout)
    q2 = to_sib(proj_of(2))
    d_zed.wait_recv()
    w4d = to_sib(mlp_of(wd, ZED))
    attend_all(5, 8)
    p_z7.wait_recv()
    q7 = to_sib(proj_of(7))
    p_z5.wait_recv()
    q5 = to_sib(proj_of(5))
    u_outer.wait_recv()
    u_z7 = send(mlp_of(wu, OUTER), mlp_of(wu, 7), zin)
    w3u = to_sib(mlp_of(wu, OUTER))
    attend(0, hb)
    p_z6.wait_recv()
    q6 = to_sib(proj_of(6))

    res[...] = jnp.zeros((ROWS, D), F32)
    for q in (q1, q2, q3, q4, q5, q6, q7):
        q.wait_recv()
    for slot in range(1, GROUP):
        head_copy(slot).wait_recv()

    @pl.loop(0, GROUP)
    def _(slot):
        weights = wp[pl.ds(2 * slot, 2)].reshape(2 * LANE, D)
        res[...] += nn(hb[slot], weights)

    mid = hd[0].astype(F32) + mod[2:3] * res[...]
    res[...] = mid
    xb[0] = (norm(mid) * (1.0 + mod[4:5]) + mod[3:4]).astype(BF16)
    x_inner = send(xb.at[0], xb.at[1], inner)

    acc[...] = jnp.zeros((2, ROWS, D), F32)

    def mlp(side, low, high):
        @pl.loop(low, high)
        def _(step):
            at = pl.ds(pl.multiple_of(step * CHUNK, CHUNK), CHUNK)
            v = nt(xb[side], wu[at])
            g = 0.5 * v * (1.0 + jnp.tanh(0.7978845608 * (v + 0.044715 * (v * v * v))))
            acc[side] += nn(g.astype(BF16), wd[at])

    mlp(0, 0, 2)
    u_zed.wait_recv()
    w4u = to_sib(mlp_of(wu, ZED))
    w4d.wait_recv()
    w4u.wait_recv()
    mlp(0, 2, 4)
    d_outer.wait_recv()
    d_z7 = send(mlp_of(wd, OUTER), mlp_of(wd, 7), zout)
    w3d = to_sib(mlp_of(wd, OUTER))
    x_inner.wait_recv()
    mlp(1, 0, 4)
    u_z7.wait_recv()
    w7u = to_sib(mlp_of(wu, 7))
    w3u.wait_recv()
    w3d.wait_recv()
    mlp(1, 4, 6)
    mlp(0, 4, 6)
    d_z7.wait_recv()
    w7d = to_sib(mlp_of(wd, 7))
    w7u.wait_recv()
    w7d.wait_recv()
    mlp(1, 6, 9)
    back = []
    for part in range(RCH):
        at = pl.ds(part * (ROWS // RCH), ROWS // RCH)
        rs[at] = acc[1, at].astype(BF16)
        back.append(send(rs.at[at], rr.at[at], inner))
    mlp(0, 6, 9)

    own_count = counts_ref[latent, member]
    for part in range(RCH):
        at = pl.ds(part * (ROWS // RCH), ROWS // RCH)
        back[part].wait_recv()
        total = acc[0, at] + rr[at].astype(F32)
        valid = slot_row[0 : ROWS // RCH] + part * (ROWS // RCH) < own_count
        block = jnp.where(valid, res[at] + mod[5:6] * total, 0.0).astype(BF16)
        out_blk[0, at] = block
        fin = (norm(block.astype(F32)) * (1.0 + mod[7:8]) + mod[6:7]).astype(BF16)
        scale = gd_ref[latent]
        weight = jnp.where(half == 0, scale, 1.0 - scale)
        ps[at] = weight * nn(fin, fw_ref[...])
    noise = send(ps, pr, sib)
    noise.wait_recv()
    guided = ps[...] + pr[...]
    stepped = sc_ref[latent, 0] * lat_ref[...] - sc_ref[latent, 1] * guided
    out_lat[...] = jnp.where(slot_row < own_count, stepped, 0.0)

    for copy in sent:
        copy.wait_send()
    for slot in range(1, GROUP):
        head_copy(slot).wait_send()


def shards(*args):
    vmem = pl.BlockSpec(memory_space=pltpu.VMEM)
    smem = pl.BlockSpec(memory_space=pltpu.SMEM)
    anyspace = pl.BlockSpec(memory_space=pl.ANY)
    copies = 80
    return pl.pallas_call(
        kernel,
        out_shape=(
            jax.ShapeDtypeStruct((ROWS, 16), F32),
            jax.ShapeDtypeStruct((1, ROWS, D), BF16),
        ),
        in_specs=[anyspace, vmem, smem, anyspace, anyspace, anyspace, anyspace, anyspace, vmem, smem, smem],
        out_specs=(vmem, vmem),
        scratch_shapes=[
            pltpu.VMEM((GROUP, ROWS, D), BF16),
            pltpu.VMEM((8, D), F32),
            pltpu.VMEM((D, 6 * HD), BF16),
            pltpu.VMEM((D, 2 * HD), BF16),
            pltpu.VMEM((D, UNITS), BF16),
            pltpu.VMEM((D, UNITS), BF16),
            pltpu.VMEM((D, 6 * LANE), BF16),
            pltpu.VMEM((2 * GROUP, LANE, D), BF16),
            pltpu.VMEM((4 * UNITS, D), BF16),
            pltpu.VMEM((4 * UNITS, D), BF16),
            pltpu.VMEM((GROUP * ROWS, 2 * LANE), BF16),
            pltpu.VMEM((GROUP * ROWS, 2 * LANE), BF16),
            pltpu.VMEM((GROUP * ROWS, 2 * LANE), BF16),
            pltpu.VMEM((GROUP, ROWS, 2 * LANE), BF16),
            pltpu.VMEM((GROUP, ROWS, 2 * LANE), BF16),
            pltpu.VMEM((2, ROWS, D), BF16),
            pltpu.VMEM((2, ROWS, D), F32),
            pltpu.VMEM((ROWS, D), F32),
            pltpu.VMEM((ROWS, D), BF16),
            pltpu.VMEM((ROWS, D), BF16),
            pltpu.VMEM((ROWS, 16), F32),
            pltpu.VMEM((ROWS, 16), F32),
            pltpu.SemaphoreType.DMA((6,)),
            pltpu.SemaphoreType.DMA((copies,)),
            pltpu.SemaphoreType.DMA((copies,)),
        ],
        compiler_params=pltpu.CompilerParams(
            collective_id=0, has_side_effects=True, vmem_limit_bytes=64 * 1024 * 1024 - 65536 - 2048
        ),
    )(*args)


def solution(mesh):
    placed = (
        P("tok", None),
        P("tok", None),
        P(),
        P("cfg", None, None, None),
        P("tok", None, None),
        P("tok", None, None),
        P("tok", None, None),
        P("tok", None, None),
        P(),
        P(),
        P(),
    )
    return jax.shard_map(
        shards,
        mesh=mesh,
        in_specs=placed,
        out_specs=(P("tok", None), P("cfg", "tok", None)),
        check_vma=False,
    )
```

```python
import jax
import jax.numpy as jnp
from jax import lax
from jax.experimental import pallas as pl
from jax.experimental.pallas import tpu as pltpu
from jax.sharding import PartitionSpec as P

MESH = pl.DeviceIdType.MESH
F32 = jnp.float32
BF16 = jnp.bfloat16
HD = 72
GROUP = 8
LANE = 128
ROWS = 192
D = 1152
UNITS = 576
CHUNK = 256
RCH = 2
EXP_SCALE = HD**-0.5 * 1.4426950408889634

INNER, OUTER, ZED = 1, 3, 4
WSLOT = {0: 0, 4: 1, 3: 2, 7: 3}


def nt(a, b):
    return lax.dot_general(a, b, (((1,), (1,)), ((), ())), preferred_element_type=F32)


def nn(a, b):
    return jnp.dot(a, b, preferred_element_type=F32)


def norm(v):
    center = v - jnp.mean(v, axis=-1, keepdims=True)
    spread = jnp.mean(center * center, axis=-1, keepdims=True)
    return center * lax.rsqrt(spread + 1e-06)


def kernel(
    hid_hbm, lat_ref, counts_ref, mod_hbm, wq_hbm, wp_hbm, wu_hbm, wd_hbm, fw_ref, gd_ref, sc_ref,
    out_lat, out_blk,
    hd, mod, wq_raw, wp_raw, wq, wp, wu, wd,
    qb, kb, vb, hs, hb, xb, acc, res, final, rs, rr, ps, pr,
    lsem, ssem, rsem,
):
    tok = lax.axis_index("tok")
    half = lax.axis_index("cfg")
    latent = tok // GROUP
    member = tok % GROUP
    z = (tok // 4) % 8
    zo = jnp.where(z % 2 == 1, (z + 1) % 8, (z + 7) % 8)
    zed_out = tok + (zo - z) * 4

    def flip(slot):
        bit0 = tok % 2
        bit1 = (tok // 2) % 2
        bit2 = (tok // 4) % 2
        s0, s1, s2 = slot % 2, (slot // 2) % 2, (slot // 4) % 2
        return tok + s0 * (1 - 2 * bit0) + 2 * s1 * (1 - 2 * bit1) + 4 * s2 * (1 - 2 * bit2)

    inner = {"cfg": half, "tok": flip(INNER)}
    outer = {"cfg": half, "tok": flip(OUTER)}
    zin = {"cfg": half, "tok": flip(ZED)}
    zout = {"cfg": half, "tok": zed_out}
    sib = {"cfg": 1 - half, "tok": tok}

    loads = [
        pltpu.make_async_copy(hid_hbm, hd.at[0], lsem.at[0]),
        pltpu.make_async_copy(wp_hbm.at[0], wp_raw, lsem.at[1]),
        pltpu.make_async_copy(wu_hbm.at[0], wu.at[pl.ds(0, UNITS)], lsem.at[2]),
        pltpu.make_async_copy(wd_hbm.at[0], wd.at[pl.ds(0, UNITS)], lsem.at[3]),
        pltpu.make_async_copy(wq_hbm.at[0], wq_raw, lsem.at[4]),
        pltpu.make_async_copy(mod_hbm.at[0, latent], mod, lsem.at[5]),
    ]
    for load in loads:
        load.start()

    barrier = pltpu.get_barrier_semaphore()
    peers = [{"cfg": half, "tok": flip(s)} for s in range(1, GROUP)] + [zout, sib]
    for peer in peers:
        pl.semaphore_signal(barrier, inc=1, device_id=peer, device_id_type=MESH)
    pl.semaphore_wait(barrier, len(peers))

    sent = []
    number = [0]

    def plan(src, dst, device):
        index = number[0]
        number[0] += 1
        return pltpu.make_async_remote_copy(
            src_ref=src, dst_ref=dst, send_sem=ssem.at[index], recv_sem=rsem.at[index],
            device_id=device, device_id_type=MESH,
        )

    def send(src, dst, device):
        copy = plan(src, dst, device)
        copy.start()
        sent.append(copy)
        return copy

    def rows_of(slot, part=None):
        if part is None:
            return hd.at[slot, pl.ds(pl.multiple_of(half * 96, 16), 96)]
        return hd.at[slot, pl.ds(pl.multiple_of(half * 96 + part * 48, 16), 48)]

    def proj_of(slot):
        return wp.at[2 * slot + half, pl.ds(0, 80)]

    def mlp_of(ref, slot):
        return ref.at[pl.ds(pl.multiple_of(WSLOT[slot] * UNITS + half * 288, 16), 288)]

    def to_sib(ref):
        return send(ref, ref, sib)

    loads[0].wait()
    h_outer = send(rows_of(0), rows_of(OUTER), outer)
    h_inner = send(rows_of(0), rows_of(INNER), inner)
    h_zed = send(rows_of(0), rows_of(ZED), zin)

    wp[:, 80:LANE] = jnp.zeros((2 * GROUP, LANE - 80, D), BF16)
    loads[1].wait()
    row = lax.broadcasted_iota(jnp.int32, (160, 2 * HD), 0)
    col = lax.broadcasted_iota(jnp.int32, (160, 2 * HD), 1)
    pick = ((row < HD) & (col == row)) | ((row >= 80) & (row < 80 + HD) & (col == row - 8))
    own_proj = nn(jnp.where(pick, 1.0, 0.0).astype(BF16), wp_raw[...]).astype(BF16)
    wp[0, 0:80] = own_proj[0:80]
    wp[1, 0:80] = own_proj[80:160]
    loads[2].wait()
    loads[3].wait()

    p_outer = send(proj_of(0), proj_of(OUTER), outer)
    u_outer = send(mlp_of(wu, 0), mlp_of(wu, OUTER), outer)
    d_outer = send(mlp_of(wd, 0), mlp_of(wd, OUTER), outer)
    p_zed = send(proj_of(0), proj_of(ZED), zout)
    d_zed = send(mlp_of(wd, 0), mlp_of(wd, ZED), zout)

    loads[4].wait()
    loads[5].wait()
    row = lax.broadcasted_iota(jnp.int32, (6 * LANE, 6 * HD), 0)
    col = lax.broadcasted_iota(jnp.int32, (6 * LANE, 6 * HD), 1)
    pick = (col == (row // LANE) * HD + row % LANE) & (row % LANE < HD)
    wq[...] = nn(jnp.where(pick, 1.0, 0.0).astype(BF16), wq_raw[...]).astype(BF16)

    lane = lax.broadcasted_iota(jnp.int32, (1, 2 * LANE), 1) % LANE
    one_lane = jnp.where(lane == HD, 1.0, 0.0)
    slot_row = lax.broadcasted_iota(jnp.int32, (ROWS, 1), 0)

    def project(slot):
        x = hd[slot].astype(F32)
        a = (norm(x) * (1.0 + mod[1:2]) + mod[0:1]).astype(BF16)
        y = nt(a, wq[...])
        count = counts_ref[flip(slot) % GROUP, latent]
        bias = jnp.where(slot_row < count, 0.0, -1e30)
        at = pl.ds(pl.multiple_of(slot * ROWS, 16), ROWS)
        qb[at] = (y[:, 0:256] + one_lane).astype(BF16)
        kb[at] = (y[:, 256:512] + one_lane * bias).astype(BF16)
        vb[at] = (y[:, 512:768] + one_lane).astype(BF16)

    def project_all(slots):
        first, stride, count = slots

        @pl.loop(0, count)
        def _(i):
            project(first + i * stride)

    h_outer.wait_recv()
    h_i2 = send(rows_of(OUTER), rows_of(2), inner)
    h_z7 = send(rows_of(OUTER), rows_of(7), zin)
    s3 = to_sib(rows_of(OUTER))
    h_zed.wait_recv()
    h_i5 = send(rows_of(ZED, 0), rows_of(5, 0), inner)
    s4 = to_sib(rows_of(ZED))
    h_inner.wait_recv()
    h_z5 = send(rows_of(INNER, 1), rows_of(5, 1), zin)
    s1 = to_sib(rows_of(INNER))

    project_all((0, 1, 1))
    s3.wait_recv()
    s4.wait_recv()
    project_all((3, 1, 2))

    h_z7.wait_recv()
    h_i6 = send(rows_of(7, 0), rows_of(6, 0), inner)
    s7 = to_sib(rows_of(7))
    h_i2.wait_recv()
    h_z6 = send(rows_of(2, 1), rows_of(6, 1), zin)
    s2 = to_sib(rows_of(2))
    p_inner = send(proj_of(0), proj_of(INNER), inner)
    u_zed = send(mlp_of(wu, 0), mlp_of(wu, ZED), zin)

    s1.wait_recv()
    s2.wait_recv()
    project_all((1, 1, 2))
    h_i5.wait_recv()
    h_z5.wait_recv()
    s5 = to_sib(rows_of(5))

    p_outer.wait_recv()
    p_i2 = send(proj_of(OUTER), proj_of(2), inner)
    p_z7 = send(proj_of(OUTER), proj_of(7), zout)
    q3 = to_sib(proj_of(OUTER))
    p_zed.wait_recv()
    q4 = to_sib(proj_of(ZED))

    s7.wait_recv()
    s5.wait_recv()
    project_all((5, 2, 2))
    h_i6.wait_recv()
    h_z6.wait_recv()
    s6 = to_sib(rows_of(6))
    p_inner.wait_recv()
    p_z5 = send(proj_of(INNER), proj_of(5), zout)
    q1 = to_sib(proj_of(INNER))
    s6.wait_recv()
    project_all((6, 1, 1))

    def attend(slot, out):
        at = pl.ds(pl.multiple_of(slot * ROWS, 16), ROWS)
        for head in range(2):
            lanes = pl.ds(head * LANE, LANE)
            scores = nt(qb[at, lanes], kb[:, lanes])
            peak = jnp.max(scores, axis=-1, keepdims=True)
            probs = jnp.exp2((scores - peak) * EXP_SCALE).astype(BF16)
            o = nn(probs, vb[:, lanes])
            out[slot, :, lanes] = (o / o[:, HD : HD + 1]).astype(BF16)

    base = number[0]
    number[0] += GROUP

    def head_copy(slot):
        return pltpu.make_async_remote_copy(
            src_ref=hs.at[slot], dst_ref=hb.at[slot], send_sem=ssem.at[base + slot], recv_sem=rsem.at[base + slot],
            device_id={"cfg": half, "tok": flip(slot)}, device_id_type=MESH,
        )

    def attend_all(low, high):
        @pl.loop(low, high)
        def _(i):
            slot = GROUP - i
            attend(slot, hs)
            head_copy(slot).start()

    attend_all(1, 5)
    p_i2.wait_recv()
    p_z6 = send(proj_of(2), proj_of(6), zout)
    q2 = to_sib(proj_of(2))
    d_zed.wait_recv()
    w4d = to_sib(mlp_of(wd, ZED))
    attend_all(5, 8)
    p_z7.wait_recv()
    q7 = to_sib(proj_of(7))
    p_z5.wait_recv()
    q5 = to_sib(proj_of(5))
    u_outer.wait_recv()
    u_z7 = send(mlp_of(wu, OUTER), mlp_of(wu, 7), zin)
    w3u = to_sib(mlp_of(wu, OUTER))
    attend(0, hb)
    p_z6.wait_recv()
    q6 = to_sib(proj_of(6))

    res[...] = jnp.zeros((ROWS, D), F32)
    for q in (q1, q2, q3, q4, q5, q6, q7):
        q.wait_recv()
    for slot in range(1, GROUP):
        head_copy(slot).wait_recv()

    @pl.loop(0, GROUP)
    def _(slot):
        weights = wp[pl.ds(2 * slot, 2)].reshape(2 * LANE, D)
        res[...] += nn(hb[slot], weights)

    mid = hd[0].astype(F32) + mod[2:3] * res[...]
    res[...] = mid
    xb[0] = (norm(mid) * (1.0 + mod[4:5]) + mod[3:4]).astype(BF16)
    x_inner = send(xb.at[0], xb.at[1], inner)

    acc[...] = jnp.zeros((2, ROWS, D), F32)

    def mlp(side, low, high):
        @pl.loop(low, high)
        def _(step):
            at = pl.ds(pl.multiple_of(step * CHUNK, CHUNK), CHUNK)
            v = nt(xb[side], wu[at])
            g = 0.5 * v * (1.0 + jnp.tanh(0.7978845608 * (v + 0.044715 * (v * v * v))))
            acc[side] += nn(g.astype(BF16), wd[at])

    mlp(0, 0, 2)
    u_zed.wait_recv()
    w4u = to_sib(mlp_of(wu, ZED))
    w4d.wait_recv()
    w4u.wait_recv()
    mlp(0, 2, 4)
    d_outer.wait_recv()
    d_z7 = send(mlp_of(wd, OUTER), mlp_of(wd, 7), zout)
    w3d = to_sib(mlp_of(wd, OUTER))
    x_inner.wait_recv()
    mlp(1, 0, 4)
    u_z7.wait_recv()
    w7u = to_sib(mlp_of(wu, 7))
    w3u.wait_recv()
    w3d.wait_recv()
    mlp(1, 4, 6)
    mlp(0, 4, 6)
    d_z7.wait_recv()
    w7d = to_sib(mlp_of(wd, 7))
    w7u.wait_recv()
    w7d.wait_recv()
    mlp(1, 6, 9)
    back = []
    for part in range(RCH):
        at = pl.ds(part * (ROWS // RCH), ROWS // RCH)
        rs[at] = acc[1, at].astype(BF16)
        back.append(send(rs.at[at], rr.at[at], inner))
    mlp(0, 6, 9)

    own_count = counts_ref[member, latent]
    for part in range(RCH):
        at = pl.ds(part * (ROWS // RCH), ROWS // RCH)
        back[part].wait_recv()
        total = acc[0, at] + rr[at].astype(F32)
        valid = slot_row[0 : ROWS // RCH] + part * (ROWS // RCH) < own_count
        block = jnp.where(valid, res[at] + mod[5:6] * total, 0.0).astype(BF16)
        out_blk[0, at] = block
        fin = (norm(block.astype(F32)) * (1.0 + mod[7:8]) + mod[6:7]).astype(BF16)
        final[at] = fin
    scale = gd_ref[latent]
    weight = jnp.where(half == 0, scale, 1.0 - scale)
    ps[...] = weight * nt(fw_ref[...], final[...])
    noise = send(ps, pr, sib)
    noise.wait_recv()
    guided = ps[...] + pr[...]
    stepped = sc_ref[0, latent] * lat_ref[...] - sc_ref[1, latent] * guided
    slot_lane = lax.broadcasted_iota(jnp.int32, (1, ROWS), 1)
    out_lat[...] = jnp.where(slot_lane < own_count, stepped, 0.0)

    for copy in sent:
        copy.wait_send()
    for slot in range(1, GROUP):
        head_copy(slot).wait_send()


def shards(hidden_in, noisy_latent, piece_rows, modulation, qkv_weight, proj_weight, up_weight, down_weight, final_weight, guidance, solver_coef):
    vmem = pl.BlockSpec(memory_space=pltpu.VMEM)
    smem = pl.BlockSpec(memory_space=pltpu.SMEM)
    anyspace = pl.BlockSpec(memory_space=pl.ANY)
    copies = 80
    next_latent, block_out = pl.pallas_call(
        kernel,
        out_shape=(
            jax.ShapeDtypeStruct((16, ROWS), F32),
            jax.ShapeDtypeStruct((1, ROWS, D), BF16),
        ),
        in_specs=[anyspace, vmem, smem, anyspace, anyspace, anyspace, anyspace, anyspace, vmem, smem, smem],
        out_specs=(vmem, vmem),
        scratch_shapes=[
            pltpu.VMEM((GROUP, ROWS, D), BF16),
            pltpu.VMEM((8, D), F32),
            pltpu.VMEM((6 * HD, D), BF16),
            pltpu.VMEM((2 * HD, D), BF16),
            pltpu.VMEM((6 * LANE, D), BF16),
            pltpu.VMEM((2 * GROUP, LANE, D), BF16),
            pltpu.VMEM((4 * UNITS, D), BF16),
            pltpu.VMEM((4 * UNITS, D), BF16),
            pltpu.VMEM((GROUP * ROWS, 2 * LANE), BF16),
            pltpu.VMEM((GROUP * ROWS, 2 * LANE), BF16),
            pltpu.VMEM((GROUP * ROWS, 2 * LANE), BF16),
            pltpu.VMEM((GROUP, ROWS, 2 * LANE), BF16),
            pltpu.VMEM((GROUP, ROWS, 2 * LANE), BF16),
            pltpu.VMEM((2, ROWS, D), BF16),
            pltpu.VMEM((2, ROWS, D), F32),
            pltpu.VMEM((ROWS, D), F32),
            pltpu.VMEM((ROWS, D), BF16),
            pltpu.VMEM((ROWS, D), BF16),
            pltpu.VMEM((ROWS, D), BF16),
            pltpu.VMEM((16, ROWS), F32),
            pltpu.VMEM((16, ROWS), F32),
            pltpu.SemaphoreType.DMA((6,)),
            pltpu.SemaphoreType.DMA((copies,)),
            pltpu.SemaphoreType.DMA((copies,)),
        ],
        compiler_params=pltpu.CompilerParams(
            collective_id=0, has_side_effects=True, vmem_limit_bytes=64 * 1024 * 1024 - 65536 - 2048
        ),
    )(
        hidden_in,
        noisy_latent.T,
        piece_rows.T,
        modulation,
        qkv_weight.transpose(0, 2, 1),
        proj_weight.transpose(0, 2, 1),
        up_weight.transpose(0, 2, 1),
        down_weight.transpose(0, 2, 1),
        final_weight.T,
        guidance,
        solver_coef.T,
    )
    return next_latent.T, block_out


def solution(mesh):
    placed = (
        P("tok", None),
        P("tok", None),
        P(),
        P("cfg", None, None, None),
        P("tok", None, None),
        P("tok", None, None),
        P("tok", None, None),
        P("tok", None, None),
        P(),
        P(),
        P(),
    )
    return jax.shard_map(
        shards,
        mesh=mesh,
        in_specs=placed,
        out_specs=(P("tok", None), P("cfg", "tok", None)),
        check_vma=False,
    )
```

```python
import jax
import jax.numpy as jnp
from jax import lax
from jax.experimental import pallas as pl
from jax.experimental.pallas import tpu as pltpu
from jax.sharding import PartitionSpec as P

MESH = pl.DeviceIdType.MESH
F32 = jnp.float32
BF16 = jnp.bfloat16
HD = 72
GROUP = 8
LANE = 128
ROWS = 192
D = 1152
UNITS = 576
CHUNK = 256
RCH = 2
EXP_SCALE = HD**-0.5 * 1.4426950408889634

INNER, OUTER, ZED = 1, 3, 4
WSLOT = {0: 0, 4: 1, 3: 2, 7: 3}


def nt(a, b):
    return lax.dot_general(a, b, (((1,), (1,)), ((), ())), preferred_element_type=F32)


def nn(a, b):
    return jnp.dot(a, b, preferred_element_type=F32)


def norm(v):
    center = v - jnp.mean(v, axis=-1, keepdims=True)
    spread = jnp.mean(center * center, axis=-1, keepdims=True)
    return center * lax.rsqrt(spread + 1e-06)


def kernel(
    hid_hbm, lat_ref, counts_ref, mod_hbm, wq_hbm, wp_hbm, wu_hbm, wd_hbm, fw_ref, gd_ref, sc_ref,
    out_lat, out_blk,
    hd, mod, wq, wp, w,
    qb, kb, vb, hs, hb, xb, acc, res, final, rs, rr, ps, pr,
    lsem, ssem, rsem,
):
    tok = lax.axis_index("tok")
    half = lax.axis_index("cfg")
    latent = tok // GROUP
    member = tok % GROUP
    z = (tok // 4) % 8
    y = tok // 32
    zo = jnp.where(z % 2 == 1, (z + 1) % 8, (z + 7) % 8)

    def flip(slot):
        bit0 = tok % 2
        bit1 = (tok // 2) % 2
        bit2 = (tok // 4) % 2
        s0, s1, s2 = slot % 2, (slot // 2) % 2, (slot // 4) % 2
        return tok + s0 * (1 - 2 * bit0) + 2 * s1 * (1 - 2 * bit1) + 4 * s2 * (1 - 2 * bit2)

    sib = {"cfg": 1 - half, "tok": tok}
    links = {
        "I": ({"cfg": half, "tok": flip(INNER)}, INNER),
        "O": ({"cfg": half, "tok": flip(OUTER)}, OUTER),
        "Z": ({"cfg": half, "tok": flip(ZED)}, ZED),
        "Q": ({"cfg": half, "tok": tok + (zo - z) * 4}, ZED),
        "+": ({"cfg": half, "tok": (tok + 32) % 128}, 0),
        "-": ({"cfg": half, "tok": (tok + 96) % 128}, 0),
    }

    loads = [
        pltpu.make_async_copy(hid_hbm, hd.at[0], lsem.at[0]),
        pltpu.make_async_copy(mod_hbm.at[0, latent], mod, lsem.at[1]),
        pltpu.make_async_copy(wu_hbm.at[0], w.at[0, pl.ds(0, UNITS)], lsem.at[2]),
        pltpu.make_async_copy(wd_hbm.at[0], w.at[1, pl.ds(0, UNITS)], lsem.at[3]),
    ]
    loads += [
        pltpu.make_async_copy(wp_hbm.at[0, pl.ds(HD * i, HD)], wp.at[i, pl.ds(0, HD)], lsem.at[4 + i]) for i in range(2)
    ]
    loads += [
        pltpu.make_async_copy(wq_hbm.at[0, pl.ds(HD * i, HD)], wq.at[i, pl.ds(0, HD)], lsem.at[6 + i]) for i in range(6)
    ]
    for load in loads:
        load.start()

    wp[:, HD:LANE] = jnp.zeros((2 * GROUP, LANE - HD, D), BF16)
    wq[:, HD:LANE] = jnp.zeros((6, LANE - HD, D), BF16)

    barrier = pltpu.get_barrier_semaphore()
    peers = [{"cfg": half, "tok": flip(s)} for s in range(1, GROUP)] + [links[k][0] for k in "Q+-"] + [sib]
    for peer in peers:
        pl.semaphore_signal(barrier, inc=1, device_id=peer, device_id_type=MESH)
    pl.semaphore_wait(barrier, len(peers))

    sent = []
    number = [0]

    def send(src, dst, device):
        index = number[0]
        number[0] += 1
        copy = pltpu.make_async_remote_copy(
            src_ref=src, dst_ref=dst, send_sem=ssem.at[index], recv_sem=rsem.at[index],
            device_id=device, device_id_type=MESH,
        )
        copy.start()
        sent.append(copy)
        return copy

    def place(kind, slot, piece):
        if kind == "H":
            return hd.at[slot, pl.ds(pl.multiple_of(half * 96 + piece * 48, 16), 48)]
        if kind == "P":
            return wp.at[2 * slot + half, pl.ds(0, HD)]
        at = pl.multiple_of(WSLOT[slot] * UNITS + half * 288 + (piece % 2) * 144, 16)
        return w.at[(piece // 2 + y) % 2, pl.ds(at, 144)]

    coming = {}
    shared = {}

    def got(kind, slot, piece):
        copy = coming.pop((kind, slot, piece), None)
        if copy is not None:
            copy.wait_recv()

    def move(link, kind, slot, piece=0):
        got(kind, slot, piece)
        device, mask = links[link]
        if mask:
            key, dst = (kind, slot ^ mask, piece), place(kind, slot ^ mask, piece)
        else:
            key, dst = (kind, slot, (piece + 2) % 4), place(kind, slot, piece)
        coming[key] = send(place(kind, slot, piece), dst, device)

    def share(kind, slot, *pieces):
        for piece in pieces:
            got(kind, slot, piece)
        if kind == "H":
            ref = hd.at[slot, pl.ds(pl.multiple_of(half * 96, 16), 96)]
            shared.setdefault((kind, slot), []).append(send(ref, ref, sib))
        else:
            for piece in pieces:
                ref = place(kind, slot, piece)
                shared.setdefault((kind, slot), []).append(send(ref, ref, sib))

    def have(kind, slot):
        for copy in shared.pop((kind, slot)):
            copy.wait_recv()

    loads[0].wait()
    move("I", "H", 0, 0)
    move("O", "H", 0, 1)
    move("Z", "H", 0, 1)
    move("I", "H", 0, 1)
    move("O", "H", 0, 0)
    move("Z", "H", 0, 0)
    for load in loads[1:]:
        load.wait()
    move("Q", "W", 0, 0)

    lane = lax.broadcasted_iota(jnp.int32, (1, 2 * LANE), 1) % LANE
    one_lane = jnp.where(lane == HD, 1.0, 0.0)
    slot_row = lax.broadcasted_iota(jnp.int32, (ROWS, 1), 0)

    def project(slot):
        x = hd[slot].astype(F32)
        a = (norm(x) * (1.0 + mod[1:2]) + mod[0:1]).astype(BF16)
        y = nt(a, wq[...].reshape(6 * LANE, D))
        count = counts_ref[flip(slot) % GROUP, latent]
        bias = jnp.where(slot_row < count, 0.0, -1e30)
        at = pl.ds(pl.multiple_of(slot * ROWS, 16), ROWS)
        qb[at] = (y[:, 0:256] + one_lane).astype(BF16)
        kb[at] = (y[:, 256:512] + one_lane * bias).astype(BF16)
        vb[at] = (y[:, 512:768] + one_lane).astype(BF16)

    def project_all(first, stride, count):
        @pl.loop(0, count)
        def _(i):
            project(first + i * stride)

    project_all(0, 1, 1)
    move("I", "H", 3, 1)
    move("Z", "H", 3, 1)
    move("O", "H", 1, 0)
    move("I", "H", 4, 0)
    move("O", "H", 4, 0)
    move("Z", "H", 1, 1)
    share("H", 3, 0, 1)
    share("H", 1, 0, 1)
    share("H", 4, 0, 1)
    move("Q", "W", 0, 3)
    move("I", "H", 7, 1)
    move("Z", "H", 2, 0)
    share("H", 2, 0, 1)
    move("O", "P", 0)
    have("H", 1)
    have("H", 3)
    project_all(1, 2, 2)
    share("H", 7, 0, 1)
    share("H", 5, 0, 1)
    move("+", "W", 4, 0)
    share("W", 4, 0)
    move("I", "P", 0)
    move("O", "W", 0, 0)
    have("H", 4)
    have("H", 2)
    project_all(2, 2, 2)
    share("H", 6, 0, 1)
    move("Q", "P", 0)
    have("H", 7)
    have("H", 5)
    project_all(5, 2, 2)
    move("Z", "P", 3)
    move("I", "P", 3)
    share("P", 3, 0)
    have("H", 6)
    project_all(6, 1, 1)
    move("Z", "P", 1)
    share("P", 1, 0)
    move("+", "W", 4, 3)
    share("W", 4, 3, 2)

    def attend(slot, out):
        at = pl.ds(pl.multiple_of(slot * ROWS, 16), ROWS)
        for head in range(2):
            lanes = pl.ds(head * LANE, LANE)
            scores = nt(qb[at, lanes], kb[:, lanes])
            peak = jnp.max(scores, axis=-1, keepdims=True)
            probs = jnp.exp2((scores - peak) * EXP_SCALE).astype(BF16)
            o = nn(probs, vb[:, lanes])
            out[slot, :, lanes] = (o / o[:, HD : HD + 1]).astype(BF16)

    base = number[0]
    number[0] += GROUP

    def head_copy(slot):
        return pltpu.make_async_remote_copy(
            src_ref=hs.at[slot], dst_ref=hb.at[slot], send_sem=ssem.at[base + slot], recv_sem=rsem.at[base + slot],
            device_id={"cfg": half, "tok": flip(slot)}, device_id_type=MESH,
        )

    def attend_all(first, stride, count):
        @pl.loop(0, count)
        def _(i):
            slot = first + i * stride
            attend(slot, hs)
            head_copy(slot).start()

    attend_all(7, -4, 2)
    move("I", "P", 7)
    share("P", 7, 0)
    share("P", 4, 0)
    attend_all(6, -4, 2)
    move("O", "W", 0, 1)
    share("P", 2, 0)
    move("Q", "W", 3, 0)
    move("-", "W", 3, 0)
    share("W", 3, 0)
    attend_all(5, -4, 2)
    share("P", 5, 0)
    attend_all(4, 1, 1)
    move("O", "W", 4, 3)
    share("P", 6, 0)
    share("W", 4, 1)
    attend(0, hb)

    res[...] = jnp.zeros((ROWS, D), F32)
    move("Q", "W", 3, 1)
    move("-", "W", 3, 1)
    share("W", 3, 1)
    for slot in range(1, GROUP):
        have("P", slot)
    for slot in range(1, GROUP):
        head_copy(slot).wait_recv()

    @pl.loop(0, GROUP)
    def _(slot):
        weights = wp[pl.ds(2 * slot, 2)].reshape(2 * LANE, D)
        res[...] += nn(hb[slot], weights)

    mid = hd[0].astype(F32) + mod[2:3] * res[...]
    res[...] = mid
    xb[0] = (norm(mid) * (1.0 + mod[4:5]) + mod[3:4]).astype(BF16)
    inner = links["I"][0]
    parts = [pl.ds(part * (ROWS // RCH), ROWS // RCH) for part in range(RCH)]
    x_inner = [send(xb.at[0, at], xb.at[1, at], inner) for at in parts]

    acc[...] = jnp.zeros((2, ROWS, D), F32)

    def mlp(side, rows, low, high):
        @pl.loop(low, high)
        def _(step):
            at = pl.ds(pl.multiple_of(step * CHUNK, CHUNK), CHUNK)
            v = nt(xb[side, rows], w[0, at])
            g = 0.5 * v * (1.0 + jnp.tanh(0.7978845608 * (v + 0.044715 * (v * v * v))))
            acc[side, rows] += nn(g.astype(BF16), w[1, at])

    everything = pl.ds(0, ROWS)
    mlp(0, everything, 0, 2)
    have("W", 4)
    move("+", "W", 7, 0)
    share("W", 7, 0)
    mlp(0, everything, 2, 4)
    share("W", 3, 2)
    x_inner[0].wait_recv()
    mlp(1, parts[0], 0, 4)
    share("W", 3, 3)
    share("W", 7, 1, 3, 2)
    have("W", 3)
    mlp(0, everything, 4, 6)
    have("W", 7)
    back = []
    for part, at in enumerate(parts):
        if part == 0:
            mlp(1, at, 4, 9)
        else:
            x_inner[part].wait_recv()
            mlp(1, at, 0, 9)
        rs[at] = acc[1, at].astype(BF16)
        back.append(send(rs.at[at], rr.at[at], inner))
    mlp(0, everything, 6, 9)

    own_count = counts_ref[member, latent]
    for part in range(RCH):
        at = pl.ds(part * (ROWS // RCH), ROWS // RCH)
        back[part].wait_recv()
        total = acc[0, at] + rr[at].astype(F32)
        valid = slot_row[0 : ROWS // RCH] + part * (ROWS // RCH) < own_count
        block = jnp.where(valid, res[at] + mod[5:6] * total, 0.0).astype(BF16)
        out_blk[0, at] = block
        fin = (norm(block.astype(F32)) * (1.0 + mod[7:8]) + mod[6:7]).astype(BF16)
        final[at] = fin
    scale = gd_ref[latent]
    weight = jnp.where(half == 0, scale, 1.0 - scale)
    ps[...] = weight * nt(fw_ref[...], final[...])
    noise = send(ps, pr, sib)
    noise.wait_recv()
    guided = ps[...] + pr[...]
    stepped = sc_ref[0, latent] * lat_ref[...] - sc_ref[1, latent] * guided
    slot_lane = lax.broadcasted_iota(jnp.int32, (1, ROWS), 1)
    out_lat[...] = jnp.where(slot_lane < own_count, stepped, 0.0)

    assert not coming and not shared
    for copy in sent:
        copy.wait_send()
    for slot in range(1, GROUP):
        head_copy(slot).wait_send()


def shards(hidden_in, noisy_latent, piece_rows, modulation, qkv_weight, proj_weight, up_weight, down_weight, final_weight, guidance, solver_coef):
    vmem = pl.BlockSpec(memory_space=pltpu.VMEM)
    smem = pl.BlockSpec(memory_space=pltpu.SMEM)
    anyspace = pl.BlockSpec(memory_space=pl.ANY)
    copies = 80
    next_latent, block_out = pl.pallas_call(
        kernel,
        out_shape=(
            jax.ShapeDtypeStruct((16, ROWS), F32),
            jax.ShapeDtypeStruct((1, ROWS, D), BF16),
        ),
        in_specs=[anyspace, vmem, smem, anyspace, anyspace, anyspace, anyspace, anyspace, vmem, smem, smem],
        out_specs=(vmem, vmem),
        scratch_shapes=[
            pltpu.VMEM((GROUP, ROWS, D), BF16),
            pltpu.VMEM((8, D), F32),
            pltpu.VMEM((6, LANE, D), BF16),
            pltpu.VMEM((2 * GROUP, LANE, D), BF16),
            pltpu.VMEM((2, 4 * UNITS, D), BF16),
            pltpu.VMEM((GROUP * ROWS, 2 * LANE), BF16),
            pltpu.VMEM((GROUP * ROWS, 2 * LANE), BF16),
            pltpu.VMEM((GROUP * ROWS, 2 * LANE), BF16),
            pltpu.VMEM((GROUP, ROWS, 2 * LANE), BF16),
            pltpu.VMEM((GROUP, ROWS, 2 * LANE), BF16),
            pltpu.VMEM((2, ROWS, D), BF16),
            pltpu.VMEM((2, ROWS, D), F32),
            pltpu.VMEM((ROWS, D), F32),
            pltpu.VMEM((ROWS, D), BF16),
            pltpu.VMEM((ROWS, D), BF16),
            pltpu.VMEM((ROWS, D), BF16),
            pltpu.VMEM((16, ROWS), F32),
            pltpu.VMEM((16, ROWS), F32),
            pltpu.SemaphoreType.DMA((12,)),
            pltpu.SemaphoreType.DMA((copies,)),
            pltpu.SemaphoreType.DMA((copies,)),
        ],
        compiler_params=pltpu.CompilerParams(
            collective_id=0, has_side_effects=True, vmem_limit_bytes=64 * 1024 * 1024 - 65536 - 2048
        ),
    )(
        hidden_in,
        noisy_latent.T,
        piece_rows.T,
        modulation,
        qkv_weight.transpose(0, 2, 1),
        proj_weight.transpose(0, 2, 1),
        up_weight.transpose(0, 2, 1),
        down_weight.transpose(0, 2, 1),
        final_weight.T,
        guidance,
        solver_coef.T,
    )
    return next_latent.T, block_out


def solution(mesh):
    placed = (
        P("tok", None),
        P("tok", None),
        P(),
        P("cfg", None, None, None),
        P("tok", None, None),
        P("tok", None, None),
        P("tok", None, None),
        P("tok", None, None),
        P(),
        P(),
        P(),
    )
    return jax.shard_map(
        shards,
        mesh=mesh,
        in_specs=placed,
        out_specs=(P("tok", None), P("cfg", "tok", None)),
        check_vma=False,
    )
```
